32 devices in a mesh: atoms: 8 (over z, y), sig: 4 (over x, core).
Axes of the slice: x: 2, y: 2, z: 4, core: 2. Of those that a mesh axis runs over, the one named last changes fastest.
Arguments:
- signals: bfloat16 [1024, 512], P(None, 'sig'), may hold values from -6 to 6
- dictionary: bfloat16 [1024, 4096], P(None, ('atoms', 'sig')), may hold values from -0.1875 to 0.1875
- selected: int32 [2, 4], P(None, 'sig'), may hold values from 0 to 63
- inverses: bfloat16 [2, 4, 64, 64], P(None, 'sig'), may hold values from -0.14 to 1.14
Outputs:
- correlations: bfloat16 [4096, 512], P('atoms', 'sig')
- coefficients: bfloat16 [2, 64, 512], P(None, None, 'sig')
- peak: float32 [512], P('sig')
The draws below stay inside these ranges and needn't reach their ends.
All inputs are finite; a program needn't handle non-finite values.
Results may differ from the reference program's by a relative error of at most 0.006.
Values may be sent and summed in bfloat16 or wider, within the bound.
No kernel may reach another device: no remote copies, remote signals or barrier semaphores. Data moves between devices by JAX's collectives and lax.ppermute only.
A program may use at most 128 MiB of HBM per device.

```python
import math
import jax
import jax.numpy as jnp
import numpy as np
from jax import lax

L = 1024
BLK = 64
SB = 128
STEPS = 2
ATOMS = 4096
SIGNALS = 512
NBLK = 64
NSB = 4


def draw_inverses(key, part):
    shape = (STEPS, NSB, BLK, BLK)
    noise = jax.random.truncated_normal(key, -3.0, 3.0, shape, jnp.float32) * (0.35 / 8.0)
    identity = jnp.eye(BLK, dtype=jnp.float32)
    return (identity + noise).astype(jnp.bfloat16)


def place_ends(values, own_key, low, top_value):
    longest = values.shape.index(max(values.shape))
    spots = []
    for shift in (0, 1):
        where = [jax.random.randint(jax.random.fold_in(own_key, axis), (), 0, length) for axis, length in enumerate(values.shape)]
        where[longest] = (where[longest] + shift) % values.shape[longest]
        spots.append(tuple(where))
    return values.at[spots[0]].set(low).at[spots[1]].set(top_value)


def block_levels(rng, shape, split, smallest, top_value):
    factor_of, own = 1.0, jax.random.fold_in(rng, 6)
    for axis_at, blocks in split:
        draws = jnp.exp(jax.random.uniform(jax.random.fold_in(own, axis_at), (blocks,), jnp.float32, smallest / len(split), top_value / len(split)))
        factor_of = factor_of * jnp.repeat(draws, shape[axis_at] // blocks).reshape([-1 if axis == axis_at else 1 for axis in range(len(shape))])
    return factor_of


def cumulative_ranks(number_of, slope):
    portions = [(1 << 20) // math.isqrt(standing ** slope) + 1 for standing in range(1, number_of + 1)]
    spread = 1 + sum(portions) // (1 << 30)
    return np.cumsum(np.array([max(1, weight // spread) for weight in portions]))


def ranked(key, shape, amount, slope):
    listing = cumulative_ranks(amount, slope)
    ticket = jax.random.randint(jax.random.fold_in(key, 1), shape, 0, int(listing[amount - 1]))
    grade = jnp.searchsorted(jnp.asarray(listing, jnp.int32), ticket, side="right")
    return jax.random.permutation(jax.random.fold_in(key, 2), amount)[grade].astype(jnp.int32)


def normal_values(stream_key, shape, scale, bound, cuts=(), kind=jnp.bfloat16):
    drawn = jax.random.normal(stream_key, shape, jnp.float32) * scale
    if len(cuts) > 0:
        drawn = block_levels(stream_key, shape, cuts, -0.22, 0.18) * drawn
    return jnp.clip(drawn, min=-bound, max=bound).astype(kind)


def setup_inputs(seed: int = 0) -> dict:
    splits = jax.random.split(jax.random.key(seed), 5)
    signals = normal_values(splits[0], (L, SIGNALS), 1.0, 6.0, ((1, 4),))
    dictionary = normal_values(splits[1], (L, ATOMS), L ** -0.5, 0.1875, ((1, 32),))
    selected = place_ends(ranked(splits[2], (STEPS, NSB), NBLK, 2), jax.random.fold_in(splits[2], 3), 0, NBLK - 1).astype(jnp.int32)
    inverses = draw_inverses(jax.random.fold_in(splits[4], 71), 0)
    return {"signals": signals, "dictionary": dictionary, "selected": selected, "inverses": inverses}


def reference(signals, dictionary, selected, inverses):
    block_total = signals.shape[1] // SB

    def encode(slot):
        columns = lax.dynamic_slice_in_dim(signals, slot * SB, SB, 1)
        correlation = jnp.dot(dictionary.T, columns, preferred_element_type=jnp.float32)
        weights_list = []
        for step in range(STEPS):
            block_id = selected[step, slot]
            start = (block_id * BLK).astype(jnp.int32)
            atom_block = lax.dynamic_slice_in_dim(dictionary, start, BLK, 1)
            rows_block = lax.dynamic_slice_in_dim(correlation, start, BLK, 0)
            weights_block = jnp.dot(inverses[step, slot].astype(jnp.float32), rows_block,
                                    precision=lax.Precision.HIGHEST,
                                    preferred_element_type=jnp.float32).astype(jnp.bfloat16)
            gram_panel = jnp.dot(dictionary.T, atom_block, preferred_element_type=jnp.float32).astype(jnp.bfloat16)
            correlation = correlation - jnp.dot(gram_panel, weights_block, preferred_element_type=jnp.float32)
            weights_list.append(weights_block)
        largest = jnp.max(jnp.abs(correlation), axis=0)
        return correlation.astype(jnp.bfloat16), jnp.stack(weights_list), largest

    outputs = lax.map(encode, jnp.arange(block_total, dtype=jnp.int32))
    correlation_all, weights_all, largest_all = outputs
    atom_total = dictionary.shape[1]
    correlations = jnp.transpose(correlation_all, (1, 0, 2)).reshape(atom_total, block_total * SB)
    coefficients = jnp.transpose(weights_all, (1, 2, 0, 3)).reshape(STEPS, BLK, block_total * SB)
    peak = largest_all.reshape(block_total * SB)
    return correlations, coefficients, peak
```

```python
import functools

import jax
import jax.numpy as jnp
from jax import lax
from jax.experimental import pallas as pl
from jax.experimental.pallas import tpu as pltpu
from jax.sharding import PartitionSpec as P

BLK = 64
SB = 128
STEPS = 2

VMEM = pl.BlockSpec(memory_space=pltpu.VMEM)
SMEM = pl.BlockSpec(memory_space=pltpu.SMEM)


def swap(block, axis, size, mask):
    return lax.ppermute(block, axis, [(i, i ^ mask) for i in range(size)])


def matmul(a, b):
    return jnp.dot(a, b, preferred_element_type=jnp.float32)


def pick_kernel(tags, selected, homes, *refs):
    pieces, out = refs[:-1], refs[-1]
    row = lax.broadcasted_iota(jnp.int32, (SB, STEPS * BLK), 0)
    column = lax.broadcasted_iota(jnp.int32, (SB, STEPS * BLK), 1)
    wanted = jnp.where(column < BLK, selected[0, 0] * BLK, selected[1, 0] * BLK - BLK) + column
    total = jnp.zeros(out.shape, jnp.float32)
    for tag, piece in zip(tags, pieces):
        hot = (row + homes[tag] * SB == wanted).astype(jnp.float32).astype(jnp.bfloat16)
        total += matmul(piece[...], hot)
    out[...] = total.astype(jnp.bfloat16)


def pick(selected, homes, tags, pieces):
    return pl.pallas_call(
        functools.partial(pick_kernel, tags),
        out_shape=jax.ShapeDtypeStruct((pieces[0].shape[0], STEPS * BLK), jnp.bfloat16),
        in_specs=[SMEM, SMEM] + [VMEM] * len(pieces),
        out_specs=VMEM,
    )(selected, homes, *pieces)


def exact(matrix, rows):
    high = rows.astype(jnp.bfloat16)
    rest = rows - high.astype(jnp.float32)
    middle = rest.astype(jnp.bfloat16)
    low = (rest - middle.astype(jnp.float32)).astype(jnp.bfloat16)
    return matmul(matrix, low) + matmul(matrix, middle) + matmul(matrix, high)


def finish_kernel(n_terms, n_halves, own, spots, inverses, signals, *refs):
    terms = [refs[i * n_halves : (i + 1) * n_halves] for i in range(n_terms)]
    pieces = refs[n_terms * n_halves : -3]
    corr_out, coef_out, peak_out = refs[-3:]
    halves = []
    for h in range(n_halves):
        total = terms[0][h][...]
        for term in terms[1:]:
            total = total + term[h][...]
        halves.append(total)
    chosen = jnp.concatenate(halves, 0) if n_halves > 1 else halves[0]
    chosen_t = chosen.T
    signals_t = signals[...].T
    rows = matmul(chosen_t, signals[...])
    gram = matmul(chosen_t, chosen).astype(jnp.bfloat16)
    first = exact(inverses[0, 0], rows[:BLK]).astype(jnp.bfloat16)
    rows_next = rows[BLK:] - matmul(gram[BLK:, :BLK], first)
    second = exact(inverses[1, 0], rows_next).astype(jnp.bfloat16)
    coef_out[0] = first
    coef_out[1] = second
    weights_t = jnp.concatenate([first, second], 0).T
    left = jnp.concatenate([signals_t, chosen_t], 0)
    best = jnp.zeros((SB, SB), jnp.float32)
    for i, piece in enumerate(pieces):
        both = matmul(left, piece[...])
        panel_t = both[SB:].astype(jnp.bfloat16)
        corr_t = both[:SB] - matmul(weights_t, panel_t)
        if i < own:
            start = pl.multiple_of(spots[i] * SB, SB)
            corr_out[pl.ds(start, SB), :] = corr_t.T.astype(jnp.bfloat16)
        best = jnp.maximum(best, jnp.abs(corr_t))
    peak_out[...] = jnp.max(best.T, axis=0, keepdims=True)


def finish(spots, inverses, signals, terms, pieces, own):
    n_halves = len(terms[0])
    flat = [half for term in terms for half in term]
    return pl.pallas_call(
        functools.partial(finish_kernel, len(terms), n_halves, own),
        out_shape=(
            jax.ShapeDtypeStruct((own * SB, SB), jnp.bfloat16),
            jax.ShapeDtypeStruct((STEPS, BLK, SB), jnp.bfloat16),
            jax.ShapeDtypeStruct((1, SB), jnp.float32),
        ),
        in_specs=[SMEM] + [VMEM] * (2 + len(flat) + len(pieces)),
        out_specs=(VMEM, VMEM, VMEM),
    )(spots, inverses, signals, *flat, *pieces)


def shards(n_atoms, n_sig, signals, dictionary, selected, inverses):
    me = lax.axis_index("sig")
    group = lax.axis_index("atoms")
    pieces = {0: dictionary}
    bit = n_sig // 2
    while bit:
        for mask in list(pieces):
            pieces[mask | bit] = swap(pieces[mask], "sig", n_sig, bit)
        bit //= 2
    masks = sorted(pieces)
    spots = jnp.stack([me ^ mask for mask in masks])
    listed = [pieces[mask] for mask in masks]
    chosen = pick(selected, group * n_sig + spots, list(range(n_sig)), listed)
    bit = 1
    while bit < n_atoms // 2:
        chosen = chosen + swap(chosen, "atoms", n_atoms, bit)
        bit *= 2
    terms = [[chosen], [swap(chosen, "atoms", n_atoms, bit)]]
    correlations, coefficients, peak = finish(spots, inverses, signals, terms, listed, n_sig)
    bit = 1
    while bit < n_atoms:
        peak = jnp.maximum(peak, swap(peak, "atoms", n_atoms, bit))
        bit *= 2
    return correlations, coefficients, peak[0]


def solution(mesh):
    placed = (P(None, "sig"), P(None, ("atoms", "sig")), P(None, "sig"), P(None, "sig", None, None))
    return jax.shard_map(
        functools.partial(shards, mesh.shape["atoms"], mesh.shape["sig"]),
        mesh=mesh,
        in_specs=placed,
        out_specs=(P("atoms", "sig"), P(None, None, "sig"), P("sig")),
        check_vma=False,
    )
```

```python
import functools

import jax
import jax.numpy as jnp
from jax import lax
from jax.experimental import pallas as pl
from jax.experimental.pallas import tpu as pltpu
from jax.sharding import PartitionSpec as P

BLK = 64
SB = 128
STEPS = 2

VMEM = pl.BlockSpec(memory_space=pltpu.VMEM)
SMEM = pl.BlockSpec(memory_space=pltpu.SMEM)


def swap(block, axis, size, mask):
    return lax.ppermute(block, axis, [(i, i ^ mask) for i in range(size)])


def near(array):
    return pltpu.with_memory_space_constraint(array, pltpu.VMEM)


def matmul(a, b):
    return jnp.dot(a, b, preferred_element_type=jnp.float32)


def pick_kernel(n_sig, masks, selected, *refs):
    pieces, out = refs[:-1], refs[-1]
    row = lax.broadcasted_iota(jnp.int32, (SB, STEPS * BLK), 0)
    column = lax.broadcasted_iota(jnp.int32, (SB, STEPS * BLK), 1)
    wanted = jnp.where(column < BLK, selected[0, 0] * BLK, selected[1, 0] * BLK - BLK) + column
    me, group = lax.axis_index("sig"), lax.axis_index("atoms")
    total = jnp.zeros(out.shape, jnp.float32)
    for (side, mask), piece in zip(masks, pieces):
        home = (group ^ side) * n_sig + (me ^ mask)
        hot = (row + home * SB == wanted).astype(jnp.float32).astype(jnp.bfloat16)
        total += matmul(piece[...], hot)
    out[...] = total.astype(jnp.bfloat16)


def pick(n_sig, selected, masks, pieces):
    return pl.pallas_call(
        functools.partial(pick_kernel, n_sig, masks),
        out_shape=pltpu.VMEM((pieces[0].shape[0], STEPS * BLK), jnp.bfloat16),
        in_specs=[SMEM] + [VMEM] * len(pieces),
        out_specs=VMEM,
    )(selected, *[near(piece) for piece in pieces])


def exact(matrix, rows):
    high = rows.astype(jnp.bfloat16)
    rest = rows - high.astype(jnp.float32)
    middle = rest.astype(jnp.bfloat16)
    low = (rest - middle.astype(jnp.float32)).astype(jnp.bfloat16)
    return matmul(matrix, low) + matmul(matrix, middle) + matmul(matrix, high)


def finish_kernel(shape, own, inverses, signals, *refs):
    n_halves, n_terms, n_pieces = shape
    terms = [refs[h * n_terms : (h + 1) * n_terms] for h in range(n_halves)]
    rest = refs[n_terms * n_halves : -3]
    pieces = [rest[i * n_halves : (i + 1) * n_halves] for i in range(n_pieces)]
    corr_out, coef_out, peak_out = refs[-3:]
    rows = gram = None
    lefts, start = [], 0
    for parts in terms:
        chosen = parts[0][...]
        for term in parts[1:]:
            chosen = chosen + term[...]
        depth = chosen.shape[0]
        chosen_t = chosen.T
        here = signals[start : start + depth]
        right = matmul(chosen_t, jnp.concatenate([here, chosen], 1))
        rows = right if rows is None else rows + right
        lefts.append(jnp.concatenate([here.T, chosen_t], 0))
        start += depth
    gram = rows[:, SB:].astype(jnp.bfloat16)
    rows = rows[:, :SB]
    first = exact(inverses[0, 0], rows[:BLK]).astype(jnp.bfloat16)
    rows_next = rows[BLK:] - matmul(gram[BLK:, :BLK], first)
    second = exact(inverses[1, 0], rows_next).astype(jnp.bfloat16)
    coef_out[0] = first
    coef_out[1] = second
    weights_t = jnp.concatenate([first, second], 0).T
    me = lax.axis_index("sig")
    best = jnp.zeros((SB, SB), jnp.float32)
    for i, piece in enumerate(pieces):
        both = matmul(lefts[0], piece[0][...])
        for left, part in zip(lefts[1:], piece[1:]):
            both += matmul(left, part[...])
        panel_t = both[SB:].astype(jnp.bfloat16)
        corr_t = both[:SB] - matmul(weights_t, panel_t)
        if i < own:
            at = pl.multiple_of((me ^ i) * SB, SB)
            corr_out[pl.ds(at, SB), :] = corr_t.T.astype(jnp.bfloat16)
        best = jnp.maximum(best, jnp.abs(corr_t))
    peak_out[...] = jnp.max(best.T, axis=0, keepdims=True)


def finish(inverses, signals, terms, pieces, own):
    shape = (len(terms), len(terms[0]), len(pieces))
    flat = [term for parts in terms for term in parts] + [part for piece in pieces for part in piece]
    return pl.pallas_call(
        functools.partial(finish_kernel, shape, own),
        out_shape=(
            jax.ShapeDtypeStruct((own * SB, SB), jnp.bfloat16),
            jax.ShapeDtypeStruct((STEPS, BLK, SB), jnp.bfloat16),
            pltpu.VMEM((1, SB), jnp.float32),
        ),
        in_specs=[VMEM] * (2 + len(flat)),
        out_specs=(VMEM, VMEM, VMEM),
    )(inverses, near(signals), *[near(array) for array in flat])


CHUNKS = 2
MERGE = True
ALTERNATE = True


def shards(n_atoms, n_sig, signals, dictionary, selected, inverses):
    depth = dictionary.shape[0] // CHUNKS
    parts = [dictionary[h * depth : (h + 1) * depth] for h in range(CHUNKS)]
    top = n_atoms // 2
    bits = []
    bit = 1
    while bit < (top if MERGE else n_atoms):
        bits.append(bit)
        bit *= 2
    sides = [0, top] if MERGE else [0]
    masks = list(range(n_sig))
    order_of = [(side, mask) for side in sides for mask in masks]
    held, terms = [], []
    for h, part in enumerate(parts):
        have = {}
        for side in reversed(sides):
            pieces = {0: swap(part, "atoms", n_atoms, side) if side else part}
            bit = n_sig // 2
            while bit:
                for mask in list(pieces):
                    pieces[mask | bit] = swap(pieces[mask], "sig", n_sig, bit)
                bit //= 2
            have[side] = pieces
        listed = [have[side][mask] for side in sides for mask in masks]
        held.append(listed)
        chosen = pick(n_sig, selected, order_of, listed)
        order = list(bits)
        if ALTERNATE and h % 2 and len(order) > 1:
            order[0], order[1] = order[1], order[0]
        for bit in order[:-1]:
            chosen = chosen + swap(chosen, "atoms", n_atoms, bit)
        terms.append([chosen, swap(chosen, "atoms", n_atoms, order[-1])])
    pieces = [[held[h][i] for h in range(CHUNKS)] for i in range(len(held[0]))]
    correlations, coefficients, peak = finish(inverses, signals, terms, pieces, n_sig)
    for bit in bits:
        peak = jnp.maximum(peak, swap(peak, "atoms", n_atoms, bit))
    return correlations, coefficients, peak[0]


def solution(mesh):
    placed = (P(None, "sig"), P(None, ("atoms", "sig")), P(None, "sig"), P(None, "sig", None, None))
    return jax.shard_map(
        functools.partial(shards, mesh.shape["atoms"], mesh.shape["sig"]),
        mesh=mesh,
        in_specs=placed,
        out_specs=(P("atoms", "sig"), P(None, None, "sig"), P("sig")),
        check_vma=False,
    )
```

```python
import functools

import jax
import jax.numpy as jnp
from jax import lax
from jax.experimental import pallas as pl
from jax.experimental.pallas import tpu as pltpu
from jax.sharding import PartitionSpec as P

BLK = 64
SB = 128
STEPS = 2

VMEM = pl.BlockSpec(memory_space=pltpu.VMEM)
SMEM = pl.BlockSpec(memory_space=pltpu.SMEM)
HBM = pl.BlockSpec(memory_space=pltpu.HBM)
PARAMS = pltpu.CompilerParams(vmem_limit_bytes=8 << 20)


def swap(block, axis, size, mask):
    return lax.ppermute(block, axis, [(i, i ^ mask) for i in range(size)])


def matmul(a, b):
    return jnp.dot(a, b, preferred_element_type=jnp.float32)


def near(array):
    return pltpu.with_memory_space_constraint(array, pltpu.VMEM)


def after(array, *others):
    return lax.optimization_barrier((array, *others))[0]


def hot_rows(n_sig, tags, selected):
    me, group = lax.axis_index("sig"), lax.axis_index("atoms")
    place = lax.broadcasted_iota(jnp.int32, (SB, STEPS * BLK), 0)
    column = lax.broadcasted_iota(jnp.int32, (SB, STEPS * BLK), 1)
    wanted = jnp.where(column < BLK, selected[0] * BLK, selected[1] * BLK - BLK) + column - place
    hot = []
    for side, mask in tags:
        home = ((group ^ side) * n_sig + (me ^ mask)) * SB
        hot.append((wanted == home).astype(jnp.float32).astype(jnp.bfloat16))
    return jnp.concatenate(hot, 0)


def fetch_kernel(n_sig, selected, own, mine, out):
    mine[...] = own[...]
    out[...] = matmul(own[...], hot_rows(n_sig, [(0, 0)], selected)).astype(jnp.bfloat16)


def fetch(n_sig, selected, own):
    return pl.pallas_call(
        functools.partial(fetch_kernel, n_sig),
        out_shape=(pltpu.VMEM(own.shape, jnp.bfloat16), pltpu.VMEM((own.shape[0], STEPS * BLK), jnp.bfloat16)),
        in_specs=[SMEM, VMEM],
        out_specs=(VMEM, VMEM),
        name="fetch",
        compiler_params=PARAMS,
    )(selected, own)


def pick_kernel(n_sig, selected, base, *refs):
    pieces, outs = refs[: n_sig - 1], refs[n_sig - 1 :]
    rows = jnp.concatenate([piece[...] for piece in pieces], 1)
    total = matmul(rows, hot_rows(n_sig, [(0, mask) for mask in range(1, n_sig)], selected))
    total = total.astype(jnp.bfloat16) + base[...]
    at = 0
    for out in outs:
        out[...] = total[at : at + out.shape[0]]
        at += out.shape[0]


def pick(n_sig, selected, base, pieces, depths):
    return pl.pallas_call(
        functools.partial(pick_kernel, n_sig),
        out_shape=tuple(pltpu.VMEM((depth, STEPS * BLK), jnp.bfloat16) for depth in depths),
        in_specs=[SMEM] + [VMEM] * n_sig,
        out_specs=(VMEM,) * len(depths),
        name="pick",
        compiler_params=PARAMS,
    )(selected, near(base), *[near(piece) for piece in pieces])


def ready_kernel(counts, signals, *refs):
    parts, turned, first = refs[:-2], refs[-2], refs[-1]
    at = 0
    for i, count in enumerate(counts):
        piece = jnp.concatenate([part[...] for part in parts[at : at + count]], 0).T
        at += count
        turned[i * SB : (i + 1) * SB] = piece
        first[i * SB : (i + 1) * SB] = matmul(piece, signals[...])


def ready(signals, pieces):
    parts = [near(part) for piece in pieces for part in piece]
    width = len(pieces) * SB
    return pl.pallas_call(
        functools.partial(ready_kernel, [len(piece) for piece in pieces]),
        out_shape=(
            pltpu.VMEM((width, signals.shape[0]), jnp.bfloat16),
            pltpu.VMEM((width, SB), jnp.float32),
        ),
        in_specs=[VMEM] * (1 + len(parts)),
        out_specs=(VMEM, VMEM),
        name="ready",
        compiler_params=PARAMS,
    )(near(signals), *parts)


def exact(matrix, rows):
    high = rows.astype(jnp.bfloat16)
    rest = rows - high.astype(jnp.float32)
    middle = rest.astype(jnp.bfloat16)
    low = (rest - middle.astype(jnp.float32)).astype(jnp.bfloat16)
    terms = matmul(matrix, jnp.concatenate([low, middle, high], 1))
    return terms[:, :SB] + terms[:, SB : 2 * SB] + terms[:, 2 * SB :]


def finish_kernel(n_sig, n_halves, n_sides, inverses, signals, *refs):
    corr_out, coef_out, peak_out = refs[-3:]
    halves, at = [], 0
    for count in n_halves:
        half = refs[at][...]
        for more in refs[at + 1 : at + count]:
            half = half + more[...]
        halves.append(half)
        at += count
    sides = refs[at:-3]
    chosen = jnp.concatenate(halves, 0)
    right = matmul(chosen.T, jnp.concatenate([signals[...], chosen], 1))
    rows, gram = right[:, :SB], right[:, SB:].astype(jnp.bfloat16)
    one = exact(inverses[0, 0], rows[:BLK]).astype(jnp.bfloat16)
    two = exact(inverses[1, 0], rows[BLK:] - matmul(gram[BLK:, :BLK], one)).astype(jnp.bfloat16)
    coef_out[0] = one
    coef_out[1] = two
    weights = jnp.concatenate([one, two], 0)
    me = lax.axis_index("sig")
    best = None
    for side in range(n_sides):
        turned, first = sides[2 * side], sides[2 * side + 1]
        panel = matmul(turned[...], chosen).astype(jnp.bfloat16)
        corr = first[...] - matmul(panel, weights)
        if side == 0:
            for i in range(n_sig):
                at = pl.multiple_of((me ^ i) * SB, SB)
                corr_out[pl.ds(at, SB), :] = corr[i * SB : (i + 1) * SB].astype(jnp.bfloat16)
        most = jnp.max(jnp.abs(corr), axis=0, keepdims=True)
        best = most if best is None else jnp.maximum(best, most)
    peak_out[...] = best


def finish(n_sig, inverses, signals, terms, sides):
    flat = [near(array) for group in [*terms, *sides] for array in group]
    return pl.pallas_call(
        functools.partial(finish_kernel, n_sig, [len(term) for term in terms], len(sides)),
        out_shape=(
            pltpu.VMEM((n_sig * SB, SB), jnp.bfloat16),
            pltpu.VMEM((STEPS, BLK, SB), jnp.bfloat16),
            pltpu.VMEM((1, SB), jnp.float32),
        ),
        in_specs=[VMEM] * (2 + len(flat)),
        out_specs=(VMEM, VMEM, VMEM),
        name="finish",
        compiler_params=PARAMS,
    )(near(inverses), near(signals), *flat)


def shards(n_atoms, n_sig, signals, dictionary, selected, inverses):
    selected = selected[:, 0]
    depth = dictionary.shape[0] // 2
    bits = []
    bit = 1
    while bit < n_atoms:
        bits.append(bit)
        bit *= 2
    top, twin = bits[-1], bits[0]

    def gather(piece, local):
        pieces = {0: piece}
        bit = n_sig // 2
        while bit:
            for mask in list(pieces):
                pieces[mask | bit] = swap(pieces[mask], "sig", n_sig, bit)
            pieces[0] = local
            bit //= 2
        return [pieces[mask] for mask in range(n_sig)]

    mine, base = fetch(n_sig, selected, dictionary)
    here = gather(dictionary, mine)
    beside = swap(dictionary, "atoms", n_atoms, twin)
    first, second = pick(n_sig, selected, base, here[1:], [depth, depth])
    there = gather(beside, beside)
    blocks = [first, second]
    orders = [[top] + bits[:-1], list(bits)]
    arrived = [swap(blocks[h], "atoms", n_atoms, orders[h][0]) for h in range(2)]
    for i in range(1, len(bits)):
        for h in (1, 0):
            come = after(arrived[h], blocks[1 - h]) if i > 1 or h == 0 else arrived[h]
            blocks[h] = blocks[h] + come
            arrived[h] = swap(blocks[h], "atoms", n_atoms, orders[h][i])
    sides = [ready(signals, [[piece] for piece in pieces]) for pieces in (here, there)]
    correlations, coefficients, peak = finish(n_sig, inverses, signals, [(blocks[0], arrived[0]), (blocks[1] + arrived[1],)], sides)
    for bit in bits:
        if bit != twin:
            peak = jnp.maximum(peak, swap(peak, "atoms", n_atoms, bit))
    return correlations, coefficients, peak[0]


def solution(mesh):
    placed = (P(None, "sig"), P(None, ("atoms", "sig")), P(None, "sig"), P(None, "sig", None, None))
    return jax.shard_map(
        functools.partial(shards, mesh.shape["atoms"], mesh.shape["sig"]),
        mesh=mesh,
        in_specs=placed,
        out_specs=(P("atoms", "sig"), P(None, None, "sig"), P("sig")),
        check_vma=False,
    )
```

```python
import functools

import jax
import jax.numpy as jnp
from jax import lax
from jax.experimental import pallas as pl
from jax.experimental.pallas import tpu as pltpu
from jax.sharding import PartitionSpec as P

BLK = 64
SB = 128
STEPS = 2

VMEM = pl.BlockSpec(memory_space=pltpu.VMEM)
SMEM = pl.BlockSpec(memory_space=pltpu.SMEM)
HBM = pl.BlockSpec(memory_space=pltpu.HBM)
PARAMS = pltpu.CompilerParams(vmem_limit_bytes=8 << 20)


def swap(block, axis, size, mask):
    return lax.ppermute(block, axis, [(i, i ^ mask) for i in range(size)])


def matmul(a, b):
    return jnp.dot(a, b, preferred_element_type=jnp.float32)


def near(array):
    return pltpu.with_memory_space_constraint(array, pltpu.VMEM)


def after(array, *others):
    return lax.optimization_barrier((array, *others))[0]


def hot_rows(n_sig, tags, selected):
    me, group = lax.axis_index("sig"), lax.axis_index("atoms")
    place = lax.broadcasted_iota(jnp.int32, (SB, STEPS * BLK), 0)
    column = lax.broadcasted_iota(jnp.int32, (SB, STEPS * BLK), 1)
    wanted = jnp.where(column < BLK, selected[0] * BLK, selected[1] * BLK - BLK) + column - place
    hot = []
    for side, mask in tags:
        home = ((group ^ side) * n_sig + (me ^ mask)) * SB
        hot.append((wanted == home).astype(jnp.float32).astype(jnp.bfloat16))
    return jnp.concatenate(hot, 0)


def fetch_kernel(n_sig, selected, own, mine, out):
    mine[...] = own[...]
    out[...] = matmul(own[...], hot_rows(n_sig, [(0, 0)], selected)).astype(jnp.bfloat16)


def fetch(n_sig, selected, own):
    return pl.pallas_call(
        functools.partial(fetch_kernel, n_sig),
        out_shape=(pltpu.VMEM(own.shape, jnp.bfloat16), pltpu.VMEM((own.shape[0], STEPS * BLK), jnp.bfloat16)),
        in_specs=[SMEM, VMEM],
        out_specs=(VMEM, VMEM),
        name="fetch",
        compiler_params=PARAMS,
    )(selected, own)


def pick_kernel(n_sig, selected, base, *refs):
    pieces, outs = refs[: n_sig - 1], refs[n_sig - 1 :]
    rows = jnp.concatenate([piece[...] for piece in pieces], 1)
    total = matmul(rows, hot_rows(n_sig, [(0, mask) for mask in range(1, n_sig)], selected))
    total = total.astype(jnp.bfloat16) + base[...]
    at = 0
    for out in outs:
        out[...] = total[at : at + out.shape[0]]
        at += out.shape[0]


def pick(n_sig, selected, base, pieces, depths):
    return pl.pallas_call(
        functools.partial(pick_kernel, n_sig),
        out_shape=tuple(pltpu.VMEM((depth, STEPS * BLK), jnp.bfloat16) for depth in depths),
        in_specs=[SMEM] + [VMEM] * n_sig,
        out_specs=(VMEM,) * len(depths),
        name="pick",
        compiler_params=PARAMS,
    )(selected, near(base), *[near(piece) for piece in pieces])


def ready_kernel(counts, signals, *refs):
    parts, turned, first = refs[:-2], refs[-2], refs[-1]
    at = 0
    for i, count in enumerate(counts):
        piece = jnp.concatenate([part[...] for part in parts[at : at + count]], 0).T
        at += count
        turned[i * SB : (i + 1) * SB] = piece
        first[i * SB : (i + 1) * SB] = matmul(piece, signals[...])


def ready(signals, pieces):
    parts = [near(part) for piece in pieces for part in piece]
    width = len(pieces) * SB
    return pl.pallas_call(
        functools.partial(ready_kernel, [len(piece) for piece in pieces]),
        out_shape=(
            pltpu.VMEM((width, signals.shape[0]), jnp.bfloat16),
            pltpu.VMEM((width, SB), jnp.float32),
        ),
        in_specs=[VMEM] * (1 + len(parts)),
        out_specs=(VMEM, VMEM),
        name="ready",
        compiler_params=PARAMS,
    )(near(signals), *parts)


def exact(matrix, rows):
    high = rows.astype(jnp.bfloat16)
    rest = rows - high.astype(jnp.float32)
    middle = rest.astype(jnp.bfloat16)
    low = (rest - middle.astype(jnp.float32)).astype(jnp.bfloat16)
    terms = matmul(matrix, jnp.concatenate([low, middle, high], 1))
    return terms[:, :SB] + terms[:, SB : 2 * SB] + terms[:, 2 * SB :]


def finish_kernel(n_sig, n_halves, n_sides, inverses, signals, *refs):
    corr_out, coef_out, peak_out = refs[-3:]
    halves, at = [], 0
    for count in n_halves:
        half = refs[at][...]
        for more in refs[at + 1 : at + count]:
            half = half + more[...]
        halves.append(half)
        at += count
    sides = refs[at:-3]
    chosen = jnp.concatenate(halves, 0)
    panels = [matmul(turned[...], chosen).astype(jnp.bfloat16) for turned in sides[::2]]
    right = matmul(chosen.T, jnp.concatenate([signals[...], chosen], 1))
    rows, gram = right[:, :SB], right[:, SB:].astype(jnp.bfloat16)
    one = exact(inverses[0, 0], rows[:BLK]).astype(jnp.bfloat16)
    two = exact(inverses[1, 0], rows[BLK:] - matmul(gram[BLK:, :BLK], one)).astype(jnp.bfloat16)
    coef_out[0] = one
    coef_out[1] = two
    weights = jnp.concatenate([one, two], 0)
    me = lax.axis_index("sig")
    best = None
    for side in range(n_sides):
        corr = sides[2 * side + 1][...] - matmul(panels[side], weights)
        if side == 0:
            for i in range(n_sig):
                at = pl.multiple_of((me ^ i) * SB, SB)
                corr_out[pl.ds(at, SB), :] = corr[i * SB : (i + 1) * SB].astype(jnp.bfloat16)
        most = jnp.max(jnp.abs(corr), axis=0, keepdims=True)
        best = most if best is None else jnp.maximum(best, most)
    peak_out[...] = best


def finish(n_sig, inverses, signals, terms, sides):
    flat = [near(array) for group in [*terms, *sides] for array in group]
    return pl.pallas_call(
        functools.partial(finish_kernel, n_sig, [len(term) for term in terms], len(sides)),
        out_shape=(
            pltpu.VMEM((n_sig * SB, SB), jnp.bfloat16),
            pltpu.VMEM((STEPS, BLK, SB), jnp.bfloat16),
            pltpu.VMEM((1, SB), jnp.float32),
        ),
        in_specs=[VMEM] * (2 + len(flat)),
        out_specs=(VMEM, VMEM, VMEM),
        name="finish",
        compiler_params=PARAMS,
    )(near(inverses), near(signals), *flat)


def shards(n_atoms, n_sig, signals, dictionary, selected, inverses):
    selected = selected[:, 0]
    depth = dictionary.shape[0] // 2
    bits = []
    bit = 1
    while bit < n_atoms:
        bits.append(bit)
        bit *= 2
    top, twin = bits[-1], bits[0]

    def gather(piece, local):
        pieces = {0: piece}
        bit = n_sig // 2
        while bit:
            for mask in list(pieces):
                pieces[mask | bit] = swap(pieces[mask], "sig", n_sig, bit)
            pieces[0] = local
            bit //= 2
        return [pieces[mask] for mask in range(n_sig)]

    mine, base = fetch(n_sig, selected, dictionary)
    here = gather(dictionary, mine)
    beside = swap(dictionary, "atoms", n_atoms, twin)
    first, second = pick(n_sig, selected, base, here[1:], [depth, depth])
    there = gather(beside, beside)
    blocks = [first, second]
    orders = [[top] + bits[-2::-1], bits[-2::-1] + [top]]
    arrived = [swap(blocks[h], "atoms", n_atoms, orders[h][0]) for h in range(2)]
    for i in range(1, len(bits)):
        for h in (1, 0):
            come = after(arrived[h], blocks[1 - h]) if i > 1 or h == 0 else arrived[h]
            blocks[h] = blocks[h] + come
            arrived[h] = swap(blocks[h], "atoms", n_atoms, orders[h][i])
    sides = [ready(signals, [[piece] for piece in pieces]) for pieces in (here, there)]
    correlations, coefficients, peak = finish(n_sig, inverses, signals, [(blocks[0], arrived[0]), (blocks[1] + arrived[1],)], sides)
    for bit in bits:
        if bit != twin:
            peak = jnp.maximum(peak, swap(peak, "atoms", n_atoms, bit))
    return correlations, coefficients, peak[0]


def solution(mesh):
    placed = (P(None, "sig"), P(None, ("atoms", "sig")), P(None, "sig"), P(None, "sig", None, None))
    return jax.shard_map(
        functools.partial(shards, mesh.shape["atoms"], mesh.shape["sig"]),
        mesh=mesh,
        in_specs=placed,
        out_specs=(P("atoms", "sig"), P(None, None, "sig"), P("sig")),
        check_vma=False,
    )
```

```python
import functools

import jax
import jax.numpy as jnp
from jax import lax
from jax.experimental import pallas as pl
from jax.experimental.pallas import tpu as pltpu
from jax.sharding import PartitionSpec as P

BLK = 64
SB = 128
STEPS = 2

VMEM = pl.BlockSpec(memory_space=pltpu.VMEM)
SMEM = pl.BlockSpec(memory_space=pltpu.SMEM)
HBM = pl.BlockSpec(memory_space=pltpu.HBM)
PARAMS = pltpu.CompilerParams(vmem_limit_bytes=8 << 20)


def swap(block, axis, size, mask):
    return lax.ppermute(block, axis, [(i, i ^ mask) for i in range(size)])


def matmul(a, b):
    return jnp.dot(a, b, preferred_element_type=jnp.float32)


def near(array):
    return pltpu.with_memory_space_constraint(array, pltpu.VMEM)


def after(array, *others):
    return lax.optimization_barrier((array, *others))[0]


def hot_rows(n_sig, tags, selected):
    me, group = lax.axis_index("sig"), lax.axis_index("atoms")
    place = lax.broadcasted_iota(jnp.int32, (SB, STEPS * BLK), 0)
    column = lax.broadcasted_iota(jnp.int32, (SB, STEPS * BLK), 1)
    wanted = jnp.where(column < BLK, selected[0] * BLK, selected[1] * BLK - BLK) + column - place
    hot = []
    for side, mask in tags:
        home = ((group ^ side) * n_sig + (me ^ mask)) * SB
        hot.append((wanted == home).astype(jnp.float32).astype(jnp.bfloat16))
    return jnp.concatenate(hot, 0)


def fetch_kernel(n_sig, selected, own, mine, out, hot):
    mine[...] = own[...]
    out[...] = matmul(own[...], hot_rows(n_sig, [(0, 0)], selected)).astype(jnp.bfloat16)
    hot[...] = hot_rows(n_sig, [(0, mask) for mask in range(1, n_sig)], selected)


def fetch(n_sig, selected, own):
    shapes = (own.shape, (own.shape[0], STEPS * BLK), ((n_sig - 1) * SB, STEPS * BLK))
    return pl.pallas_call(
        functools.partial(fetch_kernel, n_sig),
        out_shape=tuple(pltpu.VMEM(shape, jnp.bfloat16) for shape in shapes),
        in_specs=[SMEM, VMEM],
        out_specs=(VMEM,) * 3,
        name="fetch",
        compiler_params=PARAMS,
    )(selected, own)


def pick_kernel(starts, hot, base, *refs):
    pieces, outs = refs[: -len(starts)], refs[-len(starts) :]
    for at, out in zip(starts, outs):
        rows = slice(at, at + out.shape[0])
        total = matmul(jnp.concatenate([piece[rows] for piece in pieces], 1), hot[...])
        out[...] = total.astype(jnp.bfloat16) + base[rows]


def pick(hot, base, pieces, starts, depths):
    return pl.pallas_call(
        functools.partial(pick_kernel, starts),
        out_shape=tuple(pltpu.VMEM((depth, STEPS * BLK), jnp.bfloat16) for depth in depths),
        in_specs=[VMEM] * (2 + len(pieces)),
        out_specs=(VMEM,) * len(depths),
        name="pick",
        compiler_params=PARAMS,
    )(near(hot), near(base), *[near(piece) for piece in pieces])


def ready_kernel(counts, signals, *refs):
    parts, turned, first = refs[:-2], refs[-2], refs[-1]
    at = 0
    for i, count in enumerate(counts):
        piece = jnp.concatenate([part[...] for part in parts[at : at + count]], 0).T
        at += count
        turned[i * SB : (i + 1) * SB] = piece
        first[i * SB : (i + 1) * SB] = matmul(piece, signals[...])


def ready(signals, pieces):
    parts = [near(part) for piece in pieces for part in piece]
    width = len(pieces) * SB
    return pl.pallas_call(
        functools.partial(ready_kernel, [len(piece) for piece in pieces]),
        out_shape=(
            pltpu.VMEM((width, signals.shape[0]), jnp.bfloat16),
            pltpu.VMEM((width, SB), jnp.float32),
        ),
        in_specs=[VMEM] * (1 + len(parts)),
        out_specs=(VMEM, VMEM),
        name="ready",
        compiler_params=PARAMS,
    )(near(signals), *parts)


def exact(matrix, rows):
    high = rows.astype(jnp.bfloat16)
    rest = rows - high.astype(jnp.float32)
    middle = rest.astype(jnp.bfloat16)
    low = (rest - middle.astype(jnp.float32)).astype(jnp.bfloat16)
    terms = matmul(matrix, jnp.concatenate([low, middle, high], 1))
    return terms[:, :SB] + terms[:, SB : 2 * SB] + terms[:, 2 * SB :]


def finish_kernel(n_sig, n_halves, n_sides, inverses, signals, *refs):
    corr_out, coef_out, peak_out = refs[-3:]
    halves, at = [], 0
    for count in n_halves:
        half = refs[at][...]
        for more in refs[at + 1 : at + count]:
            half = half + more[...]
        halves.append(half)
        at += count
    sides = refs[at:-3]
    chosen = jnp.concatenate(halves, 0)
    panels = [matmul(turned[...], chosen).astype(jnp.bfloat16) for turned in sides[::2]]
    right = matmul(chosen.T, jnp.concatenate([signals[...], chosen], 1))
    rows, gram = right[:, :SB], right[:, SB:].astype(jnp.bfloat16)
    one = exact(inverses[0, 0], rows[:BLK]).astype(jnp.bfloat16)
    two = exact(inverses[1, 0], rows[BLK:] - matmul(gram[BLK:, :BLK], one)).astype(jnp.bfloat16)
    coef_out[0] = one
    coef_out[1] = two
    weights = jnp.concatenate([one, two], 0)
    me = lax.axis_index("sig")
    best = None
    for side in range(n_sides):
        corr = sides[2 * side + 1][...] - matmul(panels[side], weights)
        if side == 0:
            for i in range(n_sig):
                at = pl.multiple_of((me ^ i) * SB, SB)
                corr_out[pl.ds(at, SB), :] = corr[i * SB : (i + 1) * SB].astype(jnp.bfloat16)
        most = jnp.max(jnp.abs(corr), axis=0, keepdims=True)
        best = most if best is None else jnp.maximum(best, most)
    peak_out[...] = best


def finish(n_sig, inverses, signals, terms, sides):
    flat = [near(array) for group in [*terms, *sides] for array in group]
    return pl.pallas_call(
        functools.partial(finish_kernel, n_sig, [len(term) for term in terms], len(sides)),
        out_shape=(
            pltpu.VMEM((n_sig * SB, SB), jnp.bfloat16),
            pltpu.VMEM((STEPS, BLK, SB), jnp.bfloat16),
            pltpu.VMEM((1, SB), jnp.float32),
        ),
        in_specs=[VMEM] * (2 + len(flat)),
        out_specs=(VMEM, VMEM, VMEM),
        name="finish",
        compiler_params=PARAMS,
    )(near(inverses), near(signals), *flat)


def shards(n_atoms, n_sig, signals, dictionary, selected, inverses):
    selected = selected[:, 0]
    depth = dictionary.shape[0] // 2
    bits = []
    bit = 1
    while bit < n_atoms:
        bits.append(bit)
        bit *= 2
    top, twin = bits[-1], bits[0]

    def gather(piece, local):
        pieces = {0: piece}
        bit = n_sig // 2
        while bit:
            for mask in list(pieces):
                pieces[mask | bit] = swap(pieces[mask], "sig", n_sig, bit)
            pieces[0] = local
            bit //= 2
        return [pieces[mask] for mask in range(n_sig)]

    mine, base, hot = fetch(n_sig, selected, dictionary)
    here = gather(dictionary, mine)
    beside = swap(dictionary, "atoms", n_atoms, twin)
    first, second = pick(hot, base, here[1:], [0, depth], [depth, depth])
    there = gather(beside, beside)
    blocks = [first, second]
    orders = [[top] + bits[-2::-1], bits[-2::-1] + [top]]
    arrived = [swap(blocks[h], "atoms", n_atoms, orders[h][0]) for h in range(2)]
    for i in range(1, len(bits)):
        for h in (1, 0):
            come = after(arrived[h], blocks[1 - h]) if i > 1 or h == 0 else arrived[h]
            blocks[h] = blocks[h] + come
            arrived[h] = swap(blocks[h], "atoms", n_atoms, orders[h][i])
    sides = [ready(signals, [[piece] for piece in pieces]) for pieces in (here, there)]
    correlations, coefficients, peak = finish(n_sig, inverses, signals, [(blocks[0], arrived[0]), (blocks[1] + arrived[1],)], sides)
    for bit in bits:
        if bit != twin:
            peak = jnp.maximum(peak, swap(peak, "atoms", n_atoms, bit))
    return correlations, coefficients, peak[0]


def solution(mesh):
    placed = (P(None, "sig"), P(None, ("atoms", "sig")), P(None, "sig"), P(None, "sig", None, None))
    return jax.shard_map(
        functools.partial(shards, mesh.shape["atoms"], mesh.shape["sig"]),
        mesh=mesh,
        in_specs=placed,
        out_specs=(P("atoms", "sig"), P(None, None, "sig"), P("sig")),
        check_vma=False,
    )
```

```python
import functools

import jax
import jax.numpy as jnp
from jax import lax
from jax.experimental import pallas as pl
from jax.experimental.pallas import tpu as pltpu
from jax.sharding import PartitionSpec as P

BLK = 64
SB = 128
STEPS = 2

VMEM = pl.BlockSpec(memory_space=pltpu.VMEM)
SMEM = pl.BlockSpec(memory_space=pltpu.SMEM)
HBM = pl.BlockSpec(memory_space=pltpu.HBM)
PARAMS = pltpu.CompilerParams(vmem_limit_bytes=8 << 20)


def swap(block, axis, size, mask):
    return lax.ppermute(block, axis, [(i, i ^ mask) for i in range(size)])


def matmul(a, b):
    return jnp.dot(a, b, preferred_element_type=jnp.float32)


def near(array):
    return pltpu.with_memory_space_constraint(array, pltpu.VMEM)


def after(array, *others):
    return lax.optimization_barrier((array, *others))[0]


def hot_rows(n_sig, tags, selected):
    me, group = lax.axis_index("sig"), lax.axis_index("atoms")
    place = lax.broadcasted_iota(jnp.int32, (SB, STEPS * BLK), 0)
    column = lax.broadcasted_iota(jnp.int32, (SB, STEPS * BLK), 1)
    wanted = jnp.where(column < BLK, selected[0] * BLK, selected[1] * BLK - BLK) + column - place
    hot = []
    for side, mask in tags:
        home = ((group ^ side) * n_sig + (me ^ mask)) * SB
        hot.append((wanted == home).astype(jnp.float32).astype(jnp.bfloat16))
    return jnp.concatenate(hot, 0)


def fetch_kernel(n_sig, selected, own, mine, out, hot):
    mine[...] = own[...]
    out[...] = matmul(own[...], hot_rows(n_sig, [(0, 0)], selected)).astype(jnp.bfloat16)
    hot[...] = hot_rows(n_sig, [(0, mask) for mask in range(1, n_sig)], selected)


def fetch(n_sig, selected, own):
    shapes = (own.shape, (own.shape[0], STEPS * BLK), ((n_sig - 1) * SB, STEPS * BLK))
    return pl.pallas_call(
        functools.partial(fetch_kernel, n_sig),
        out_shape=tuple(pltpu.VMEM(shape, jnp.bfloat16) for shape in shapes),
        in_specs=[SMEM, VMEM],
        out_specs=(VMEM,) * 3,
        name="fetch",
        compiler_params=PARAMS,
    )(selected, own)


def pick_kernel(starts, hot, base, *refs):
    pieces, outs = refs[: -len(starts)], refs[-len(starts) :]
    for at, out in zip(starts, outs):
        rows = slice(at, at + out.shape[0])
        total = matmul(jnp.concatenate([piece[rows] for piece in pieces], 1), hot[...])
        out[...] = total.astype(jnp.bfloat16) + base[rows]


def pick(hot, base, pieces, starts, depths):
    return pl.pallas_call(
        functools.partial(pick_kernel, starts),
        out_shape=tuple(pltpu.VMEM((depth, STEPS * BLK), jnp.bfloat16) for depth in depths),
        in_specs=[VMEM] * (2 + len(pieces)),
        out_specs=(VMEM,) * len(depths),
        name="pick",
        compiler_params=PARAMS,
    )(near(hot), near(base), *[near(piece) for piece in pieces])


def ready_kernel(counts, signals, *refs):
    parts, turned, first = refs[:-2], refs[-2], refs[-1]
    at = 0
    for i, count in enumerate(counts):
        piece = jnp.concatenate([part[...] for part in parts[at : at + count]], 0).T
        at += count
        turned[i * SB : (i + 1) * SB] = piece
        first[i * SB : (i + 1) * SB] = matmul(piece, signals[...])


def ready(signals, pieces):
    parts = [near(part) for piece in pieces for part in piece]
    width = len(pieces) * SB
    return pl.pallas_call(
        functools.partial(ready_kernel, [len(piece) for piece in pieces]),
        out_shape=(
            pltpu.VMEM((width, signals.shape[0]), jnp.bfloat16),
            pltpu.VMEM((width, SB), jnp.float32),
        ),
        in_specs=[VMEM] * (1 + len(parts)),
        out_specs=(VMEM, VMEM),
        name="ready",
        compiler_params=PARAMS,
    )(near(signals), *parts)


def exact(matrix, rows):
    high = rows.astype(jnp.bfloat16)
    rest = rows - high.astype(jnp.float32)
    middle = rest.astype(jnp.bfloat16)
    low = (rest - middle.astype(jnp.float32)).astype(jnp.bfloat16)
    terms = matmul(matrix, jnp.concatenate([low, middle, high], 1))
    return terms[:, :SB] + terms[:, SB : 2 * SB] + terms[:, 2 * SB :]


def finish_kernel(n_sig, n_halves, n_sides, inverses, signals, *refs):
    corr_out, coef_out, peak_out = refs[-3:]
    halves, at = [], 0
    for count in n_halves:
        half = refs[at][...]
        for more in refs[at + 1 : at + count]:
            half = half + more[...]
        halves.append(half)
        at += count
    sides = refs[at:-3]
    chosen = jnp.concatenate(halves, 0)
    right = matmul(chosen.T, jnp.concatenate([signals[...], chosen], 1))
    rows, gram = right[:, :SB], right[:, SB:].astype(jnp.bfloat16)
    panels = []
    panels.append(matmul(sides[0][...], chosen).astype(jnp.bfloat16))
    one = exact(inverses[0, 0], rows[:BLK]).astype(jnp.bfloat16)
    panels.append(matmul(sides[2][...], chosen).astype(jnp.bfloat16))
    two = exact(inverses[1, 0], rows[BLK:] - matmul(gram[BLK:, :BLK], one)).astype(jnp.bfloat16)
    coef_out[0] = one
    coef_out[1] = two
    weights = jnp.concatenate([one, two], 0)
    me = lax.axis_index("sig")
    best = None
    for side in range(n_sides):
        corr = sides[2 * side + 1][...] - matmul(panels[side], weights)
        if side == 0:
            for i in range(n_sig):
                at = pl.multiple_of((me ^ i) * SB, SB)
                corr_out[pl.ds(at, SB), :] = corr[i * SB : (i + 1) * SB].astype(jnp.bfloat16)
        most = jnp.max(jnp.abs(corr), axis=0, keepdims=True)
        best = most if best is None else jnp.maximum(best, most)
    peak_out[...] = best


def finish(n_sig, inverses, signals, terms, sides):
    flat = [near(array) for group in [*terms, *sides] for array in group]
    return pl.pallas_call(
        functools.partial(finish_kernel, n_sig, [len(term) for term in terms], len(sides)),
        out_shape=(
            pltpu.VMEM((n_sig * SB, SB), jnp.bfloat16),
            pltpu.VMEM((STEPS, BLK, SB), jnp.bfloat16),
            pltpu.VMEM((1, SB), jnp.float32),
        ),
        in_specs=[VMEM] * (2 + len(flat)),
        out_specs=(VMEM, VMEM, VMEM),
        name="finish",
        compiler_params=PARAMS,
    )(near(inverses), near(signals), *flat)


def shards(n_atoms, n_sig, signals, dictionary, selected, inverses):
    selected = selected[:, 0]
    depth = dictionary.shape[0] // 2
    bits = []
    bit = 1
    while bit < n_atoms:
        bits.append(bit)
        bit *= 2
    top, twin = bits[-1], bits[0]

    def gather(piece, local):
        pieces = {0: piece}
        bit = n_sig // 2
        while bit:
            for mask in list(pieces):
                pieces[mask | bit] = swap(pieces[mask], "sig", n_sig, bit)
            pieces[0] = local
            bit //= 2
        return [pieces[mask] for mask in range(n_sig)]

    mine, base, hot = fetch(n_sig, selected, dictionary)
    here = gather(dictionary, mine)
    beside = swap(dictionary, "atoms", n_atoms, twin)
    first, second = pick(hot, base, here[1:], [0, depth], [depth, depth])
    there = gather(beside, beside)
    blocks = [first, second]
    orders = [[top] + bits[-2::-1], bits[-2::-1] + [top]]
    arrived = [swap(blocks[h], "atoms", n_atoms, orders[h][0]) for h in range(2)]
    for i in range(1, len(bits)):
        for h in (1, 0):
            come = after(arrived[h], blocks[1 - h]) if i > 1 or h == 0 else arrived[h]
            blocks[h] = blocks[h] + come
            arrived[h] = swap(blocks[h], "atoms", n_atoms, orders[h][i])
    sides = [ready(signals, [[piece] for piece in pieces]) for pieces in (here, there)]
    correlations, coefficients, peak = finish(n_sig, inverses, signals, [(blocks[0], arrived[0]), (blocks[1] + arrived[1],)], sides)
    for bit in reversed(bits):
        if bit != twin:
            peak = jnp.maximum(peak, swap(peak, "atoms", n_atoms, bit))
    return correlations, coefficients, peak[0]


def solution(mesh):
    placed = (P(None, "sig"), P(None, ("atoms", "sig")), P(None, "sig"), P(None, "sig", None, None))
    return jax.shard_map(
        functools.partial(shards, mesh.shape["atoms"], mesh.shape["sig"]),
        mesh=mesh,
        in_specs=placed,
        out_specs=(P("atoms", "sig"), P(None, None, "sig"), P("sig")),
        check_vma=False,
    )
```

```python
import functools

import jax
import jax.numpy as jnp
from jax import lax
from jax.experimental import pallas as pl
from jax.experimental.pallas import tpu as pltpu
from jax.sharding import PartitionSpec as P

BLK = 64
SB = 128
STEPS = 2

VMEM = pl.BlockSpec(memory_space=pltpu.VMEM)
SMEM = pl.BlockSpec(memory_space=pltpu.SMEM)
HBM = pl.BlockSpec(memory_space=pltpu.HBM)
PARAMS = pltpu.CompilerParams(vmem_limit_bytes=8 << 20)


def swap(block, axis, size, mask):
    return lax.ppermute(block, axis, [(i, i ^ mask) for i in range(size)])


def matmul(a, b):
    return jnp.dot(a, b, preferred_element_type=jnp.float32)


def near(array):
    return pltpu.with_memory_space_constraint(array, pltpu.VMEM)


def after(array, *others):
    return lax.optimization_barrier((array, *others))[0]


def hot_rows(n_sig, tags, selected):
    me, group = lax.axis_index("sig"), lax.axis_index("atoms")
    place = lax.broadcasted_iota(jnp.int32, (SB, STEPS * BLK), 0)
    column = lax.broadcasted_iota(jnp.int32, (SB, STEPS * BLK), 1)
    wanted = jnp.where(column < BLK, selected[0] * BLK, selected[1] * BLK - BLK) + column - place
    hot = []
    for side, mask in tags:
        home = ((group ^ side) * n_sig + (me ^ mask)) * SB
        hot.append((wanted == home).astype(jnp.float32).astype(jnp.bfloat16))
    return jnp.concatenate(hot, 0)


def fetch_kernel(n_sig, selected, own, mine, out, hot):
    mine[...] = own[...]
    out[...] = matmul(own[...], hot_rows(n_sig, [(0, 0)], selected)).astype(jnp.bfloat16)
    hot[...] = hot_rows(n_sig, [(0, mask) for mask in range(1, n_sig)], selected)


def fetch(n_sig, selected, own):
    shapes = (own.shape, (own.shape[0], STEPS * BLK), ((n_sig - 1) * SB, STEPS * BLK))
    return pl.pallas_call(
        functools.partial(fetch_kernel, n_sig),
        out_shape=tuple(pltpu.VMEM(shape, jnp.bfloat16) for shape in shapes),
        in_specs=[SMEM, VMEM],
        out_specs=(VMEM,) * 3,
        name="fetch",
        compiler_params=PARAMS,
    )(selected, own)


def pick_kernel(starts, hot, base, *refs):
    pieces, outs = refs[: -len(starts)], refs[-len(starts) :]
    for at, out in zip(starts, outs):
        rows = slice(at, at + out.shape[0])
        total = matmul(jnp.concatenate([piece[rows] for piece in pieces], 1), hot[...])
        out[...] = total.astype(jnp.bfloat16) + base[rows]


def pick(hot, base, pieces, starts, depths):
    return pl.pallas_call(
        functools.partial(pick_kernel, starts),
        out_shape=tuple(pltpu.VMEM((depth, STEPS * BLK), jnp.bfloat16) for depth in depths),
        in_specs=[VMEM] * (2 + len(pieces)),
        out_specs=(VMEM,) * len(depths),
        name="pick",
        compiler_params=PARAMS,
    )(near(hot), near(base), *[near(piece) for piece in pieces])


def ready_kernel(counts, signals, *refs):
    parts, turned, first = refs[:-2], refs[-2], refs[-1]
    at = 0
    for i, count in enumerate(counts):
        piece = jnp.concatenate([part[...] for part in parts[at : at + count]], 0).T
        at += count
        turned[i * SB : (i + 1) * SB] = piece
        first[i * SB : (i + 1) * SB] = matmul(piece, signals[...])


def ready(signals, pieces):
    parts = [near(part) for piece in pieces for part in piece]
    width = len(pieces) * SB
    return pl.pallas_call(
        functools.partial(ready_kernel, [len(piece) for piece in pieces]),
        out_shape=(
            pltpu.VMEM((width, signals.shape[0]), jnp.bfloat16),
            pltpu.VMEM((width, SB), jnp.float32),
        ),
        in_specs=[VMEM] * (1 + len(parts)),
        out_specs=(VMEM, VMEM),
        name="ready",
        compiler_params=PARAMS,
    )(near(signals), *parts)


def exact(matrix, rows):
    high = rows.astype(jnp.bfloat16)
    rest = rows - high.astype(jnp.float32)
    middle = rest.astype(jnp.bfloat16)
    low = (rest - middle.astype(jnp.float32)).astype(jnp.bfloat16)
    terms = matmul(matrix, jnp.concatenate([low, middle, high], 1))
    return terms[:, :SB] + terms[:, SB : 2 * SB] + terms[:, 2 * SB :]


def finish_kernel(n_sig, n_halves, n_sides, inverses, signals, *refs):
    corr_out, coef_out, peak_out = refs[-3:]
    halves, at = [], 0
    for count in n_halves:
        half = refs[at][...]
        for more in refs[at + 1 : at + count]:
            half = half + more[...]
        halves.append(half)
        at += count
    sides = refs[at:-3]
    chosen = jnp.concatenate(halves, 0)
    right = matmul(chosen.T, jnp.concatenate([signals[...], chosen], 1))
    rows, gram = right[:, :SB], right[:, SB:].astype(jnp.bfloat16)
    panels = []
    panels.append(matmul(sides[0][...], chosen).astype(jnp.bfloat16))
    one = exact(inverses[0, 0], rows[:BLK]).astype(jnp.bfloat16)
    panels.append(matmul(sides[2][...], chosen).astype(jnp.bfloat16))
    two = exact(inverses[1, 0], rows[BLK:] - matmul(gram[BLK:, :BLK], one)).astype(jnp.bfloat16)
    coef_out[0] = one
    coef_out[1] = two
    weights = jnp.concatenate([one, two], 0)
    me = lax.axis_index("sig")
    best = None
    for side in range(n_sides):
        corr = sides[2 * side + 1][...] - matmul(panels[side], weights)
        if side == 0:
            for i in range(n_sig):
                at = pl.multiple_of((me ^ i) * SB, SB)
                corr_out[pl.ds(at, SB), :] = corr[i * SB : (i + 1) * SB].astype(jnp.bfloat16)
        most = jnp.max(jnp.abs(corr), axis=0, keepdims=True)
        best = most if best is None else jnp.maximum(best, most)
    peak_out[...] = best


def finish(n_sig, inverses, signals, terms, sides):
    flat = [near(array) for group in [*terms, *sides] for array in group]
    return pl.pallas_call(
        functools.partial(finish_kernel, n_sig, [len(term) for term in terms], len(sides)),
        out_shape=(
            pltpu.VMEM((n_sig * SB, SB), jnp.bfloat16),
            pltpu.VMEM((STEPS, BLK, SB), jnp.bfloat16),
            pltpu.VMEM((1, SB), jnp.float32),
        ),
        in_specs=[VMEM] * (2 + len(flat)),
        out_specs=(VMEM, VMEM, VMEM),
        name="finish",
        compiler_params=PARAMS,
    )(near(inverses), near(signals), *flat)


def shards(n_atoms, n_sig, signals, dictionary, selected, inverses):
    selected = selected[:, 0]
    depth = dictionary.shape[0] // 2
    bits = []
    bit = 1
    while bit < n_atoms:
        bits.append(bit)
        bit *= 2
    top, twin = bits[-1], bits[0]

    def gather(piece, local):
        pieces = {0: piece}
        bit = n_sig // 2
        while bit:
            for mask in list(pieces):
                pieces[mask | bit] = swap(pieces[mask], "sig", n_sig, bit)
            pieces[0] = local
            bit //= 2
        return [pieces[mask] for mask in range(n_sig)]

    mine, base, hot = fetch(n_sig, selected, dictionary)
    here = gather(dictionary, mine)
    beside = swap(dictionary, "atoms", n_atoms, twin)
    first, second = pick(hot, base, here[1:], [0, depth], [depth, depth])
    there = gather(beside, beside)
    blocks = [first, second]
    orders = [[top] + bits[-2::-1], bits[-2::-1] + [top]]
    arrived = [swap(blocks[h], "atoms", n_atoms, orders[h][0]) for h in range(2)]
    for i in range(1, len(bits)):
        for h in (1, 0):
            come = after(arrived[h], blocks[1 - h]) if i == 1 and h == 0 else arrived[h]
            blocks[h] = blocks[h] + come
            arrived[h] = swap(blocks[h], "atoms", n_atoms, orders[h][i])
    sides = [ready(signals, [[piece] for piece in pieces]) for pieces in (here, there)]
    correlations, coefficients, peak = finish(n_sig, inverses, signals, [(blocks[0], arrived[0]), (blocks[1] + arrived[1],)], sides)
    for bit in reversed(bits):
        if bit != twin:
            peak = jnp.maximum(peak, swap(peak, "atoms", n_atoms, bit))
    return correlations, coefficients, peak[0]


def solution(mesh):
    placed = (P(None, "sig"), P(None, ("atoms", "sig")), P(None, "sig"), P(None, "sig", None, None))
    return jax.shard_map(
        functools.partial(shards, mesh.shape["atoms"], mesh.shape["sig"]),
        mesh=mesh,
        in_specs=placed,
        out_specs=(P("atoms", "sig"), P(None, None, "sig"), P("sig")),
        check_vma=False,
    )
```

```python
import functools

import jax
import jax.numpy as jnp
from jax import lax
from jax.experimental import pallas as pl
from jax.experimental.pallas import tpu as pltpu
from jax.sharding import PartitionSpec as P

BLK = 64
SB = 128
STEPS = 2

VMEM = pl.BlockSpec(memory_space=pltpu.VMEM)
SMEM = pl.BlockSpec(memory_space=pltpu.SMEM)
HBM = pl.BlockSpec(memory_space=pltpu.HBM)
PARAMS = pltpu.CompilerParams(vmem_limit_bytes=8 << 20)


def swap(block, axis, size, mask):
    return lax.ppermute(block, axis, [(i, i ^ mask) for i in range(size)])


def matmul(a, b):
    return jnp.dot(a, b, preferred_element_type=jnp.float32)


def near(array):
    return pltpu.with_memory_space_constraint(array, pltpu.VMEM)


def after(array, *others):
    return lax.optimization_barrier((array, *others))[0]


def hot_rows(n_sig, tags, selected):
    me, group = lax.axis_index("sig"), lax.axis_index("atoms")
    place = lax.broadcasted_iota(jnp.int32, (SB, STEPS * BLK), 0)
    column = lax.broadcasted_iota(jnp.int32, (SB, STEPS * BLK), 1)
    wanted = jnp.where(column < BLK, selected[0] * BLK, selected[1] * BLK - BLK) + column - place
    hot = []
    for side, mask in tags:
        home = ((group ^ side) * n_sig + (me ^ mask)) * SB
        hot.append((wanted == home).astype(jnp.float32).astype(jnp.bfloat16))
    return jnp.concatenate(hot, 0)


def fetch_kernel(n_sig, selected, own, mine, out, hot):
    mine[...] = own[...]
    out[...] = matmul(own[...], hot_rows(n_sig, [(0, 0)], selected)).astype(jnp.bfloat16)
    hot[...] = hot_rows(n_sig, [(0, mask) for mask in range(1, n_sig)], selected)


def fetch(n_sig, selected, own):
    shapes = (own.shape, (own.shape[0], STEPS * BLK), ((n_sig - 1) * SB, STEPS * BLK))
    return pl.pallas_call(
        functools.partial(fetch_kernel, n_sig),
        out_shape=tuple(pltpu.VMEM(shape, jnp.bfloat16) for shape in shapes),
        in_specs=[SMEM, VMEM],
        out_specs=(VMEM,) * 3,
        name="fetch",
        compiler_params=PARAMS,
    )(selected, own)


def pick_kernel(starts, hot, base, *refs):
    pieces, outs = refs[: -len(starts)], refs[-len(starts) :]
    for at, out in zip(starts, outs):
        rows = slice(at, at + out.shape[0])
        total = matmul(jnp.concatenate([piece[rows] for piece in pieces], 1), hot[...])
        out[...] = total.astype(jnp.bfloat16) + base[rows]


def pick(hot, base, pieces, starts, depths):
    return pl.pallas_call(
        functools.partial(pick_kernel, starts),
        out_shape=tuple(pltpu.VMEM((depth, STEPS * BLK), jnp.bfloat16) for depth in depths),
        in_specs=[VMEM] * (2 + len(pieces)),
        out_specs=(VMEM,) * len(depths),
        name="pick",
        compiler_params=PARAMS,
    )(near(hot), near(base), *[near(piece) for piece in pieces])


def ready_kernel(counts, signals, *refs):
    parts, turned, first = refs[:-2], refs[-2], refs[-1]
    at = 0
    for i, count in enumerate(counts):
        piece = jnp.concatenate([part[...] for part in parts[at : at + count]], 0).T
        at += count
        turned[i * SB : (i + 1) * SB] = piece
        first[i * SB : (i + 1) * SB] = matmul(piece, signals[...])


def ready(signals, pieces):
    parts = [near(part) for piece in pieces for part in piece]
    width = len(pieces) * SB
    return pl.pallas_call(
        functools.partial(ready_kernel, [len(piece) for piece in pieces]),
        out_shape=(
            pltpu.VMEM((width, signals.shape[0]), jnp.bfloat16),
            pltpu.VMEM((width, SB), jnp.float32),
        ),
        in_specs=[VMEM] * (1 + len(parts)),
        out_specs=(VMEM, VMEM),
        name="ready",
        compiler_params=PARAMS,
    )(near(signals), *parts)


def exact(matrix, rows):
    high = rows.astype(jnp.bfloat16)
    rest = rows - high.astype(jnp.float32)
    middle = rest.astype(jnp.bfloat16)
    low = (rest - middle.astype(jnp.float32)).astype(jnp.bfloat16)
    terms = matmul(matrix, jnp.concatenate([low, middle, high], 1))
    return terms[:, :SB] + terms[:, SB : 2 * SB] + terms[:, 2 * SB :]


def finish_kernel(n_sig, n_halves, n_sides, inverses, signals, *refs):
    corr_out, coef_out, peak_out = refs[-3:]
    halves, at = [], 0
    for count in n_halves:
        half = refs[at][...]
        for more in refs[at + 1 : at + count]:
            half = half + more[...]
        halves.append(half)
        at += count
    sides = refs[at:-3]
    chosen = jnp.concatenate(halves, 0)
    right = matmul(chosen.T, jnp.concatenate([signals[...], chosen], 1))
    rows, gram = right[:, :SB], right[:, SB:].astype(jnp.bfloat16)
    panels = []
    panels.append(matmul(sides[0][...], chosen).astype(jnp.bfloat16))
    one = exact(inverses[0, 0], rows[:BLK]).astype(jnp.bfloat16)
    panels.append(matmul(sides[2][...], chosen).astype(jnp.bfloat16))
    two = exact(inverses[1, 0], rows[BLK:] - matmul(gram[BLK:, :BLK], one)).astype(jnp.bfloat16)
    coef_out[0] = one
    coef_out[1] = two
    weights = jnp.concatenate([one, two], 0)
    me = lax.axis_index("sig")
    best = None
    for side in range(n_sides):
        corr = sides[2 * side + 1][...] - matmul(panels[side], weights)
        if side == 0:
            for i in range(n_sig):
                at = pl.multiple_of((me ^ i) * SB, SB)
                corr_out[pl.ds(at, SB), :] = corr[i * SB : (i + 1) * SB].astype(jnp.bfloat16)
        most = jnp.max(jnp.abs(corr), axis=0, keepdims=True)
        best = most if best is None else jnp.maximum(best, most)
    peak_out[...] = best


def finish(n_sig, inverses, signals, terms, sides):
    flat = [near(array) for group in [*terms, *sides] for array in group]
    return pl.pallas_call(
        functools.partial(finish_kernel, n_sig, [len(term) for term in terms], len(sides)),
        out_shape=(
            pltpu.VMEM((n_sig * SB, SB), jnp.bfloat16),
            pltpu.VMEM((STEPS, BLK, SB), jnp.bfloat16),
            pltpu.VMEM((1, SB), jnp.float32),
        ),
        in_specs=[VMEM] * (2 + len(flat)),
        out_specs=(VMEM, VMEM, VMEM),
        name="finish",
        compiler_params=PARAMS,
    )(near(inverses), near(signals), *flat)


def shards(n_atoms, n_sig, signals, dictionary, selected, inverses):
    selected = selected[:, 0]
    depth = dictionary.shape[0] // 2
    bits = []
    bit = 1
    while bit < n_atoms:
        bits.append(bit)
        bit *= 2
    top, twin = bits[-1], bits[1]

    def gather(piece, local):
        pieces = {0: piece}
        bit = n_sig // 2
        while bit:
            for mask in list(pieces):
                pieces[mask | bit] = swap(pieces[mask], "sig", n_sig, bit)
            pieces[0] = local
            bit //= 2
        return [pieces[mask] for mask in range(n_sig)]

    mine, base, hot = fetch(n_sig, selected, dictionary)
    here = gather(dictionary, mine)
    beside = swap(dictionary, "atoms", n_atoms, twin)
    first, second = pick(hot, base, here[1:], [0, depth], [depth, depth])
    there = gather(beside, beside)
    blocks = [first, second]
    orders = [[top] + bits[-2::-1], bits[-2::-1] + [top]]
    arrived = [swap(blocks[h], "atoms", n_atoms, orders[h][0]) for h in range(2)]
    for i in range(1, len(bits)):
        for h in (1, 0):
            come = after(arrived[h], blocks[1 - h]) if i == 1 and h == 0 else arrived[h]
            blocks[h] = blocks[h] + come
            arrived[h] = swap(blocks[h], "atoms", n_atoms, orders[h][i])
    sides = [ready(signals, [[piece] for piece in pieces]) for pieces in (here, there)]
    correlations, coefficients, peak = finish(n_sig, inverses, signals, [(blocks[0], arrived[0]), (blocks[1] + arrived[1],)], sides)
    for bit in reversed(bits):
        if bit != twin:
            peak = jnp.maximum(peak, swap(peak, "atoms", n_atoms, bit))
    return correlations, coefficients, peak[0]


def solution(mesh):
    placed = (P(None, "sig"), P(None, ("atoms", "sig")), P(None, "sig"), P(None, "sig", None, None))
    return jax.shard_map(
        functools.partial(shards, mesh.shape["atoms"], mesh.shape["sig"]),
        mesh=mesh,
        in_specs=placed,
        out_specs=(P("atoms", "sig"), P(None, None, "sig"), P("sig")),
        check_vma=False,
    )
```
